32 devices in a mesh: front: 4 (over y, core), row: 8 (over z, x).
Axes of the slice: x: 2, y: 2, z: 4, core: 2. Of those that a mesh axis runs over, the one named last changes fastest.
Arguments:
- rhs_diag: float32 [4, 32, 2048], P('front', None, 'row'), may hold values from -6 to 6
- rhs_off: float32 [4, 32, 12288], P('front', None, 'row'), may hold values from -6 to 6
- diag_factor: float32 [4, 2048, 2048], P('front', 'row'), may hold values from -0.125 to 0.125
- off_factor: float32 [4, 12288, 2048], P('front', 'row'), may hold values from -0.125 to 0.125
- diag_inverse: float32 [4, 4, 512, 512], P('front')
- pattern: int32 [4, 4, 96], P('front', None, 'row'), may hold values 0 or 1
- upd_vals: float32 [32, 4, 8, 4, 8, 128], P(None, 'front', 'row'), may hold values from -4 to 4
- upd_rows: int32 [4, 8, 4, 8, 128], P('front', 'row'), may hold values from 0 to 1791
Outputs:
- solved: float32 [4, 32, 2048], P('front', None, 'row')
- remainder: float32 [4, 32, 12288], P('front', None, 'row')
The draws below stay inside these ranges and needn't reach their ends.
Inputs may be any that keep to these rules, and one draw needn't show every extreme that they name: `upd_rows`: relative rows of the receiving row block: below 256 a window row, else a row below the window; several entries may name one row.
All inputs are finite; a program needn't handle non-finite values. No bound on the sum of `pattern` on one device may be relied on, other than what follows from the above.
Results may differ from the reference program's by a relative error of at most 0.0001.
Values sent between devices are 32-bit elements; how exact they have to be, the bound alone decides.
A program may use at most 128 MiB of HBM per device.

```python
import jax
import jax.numpy as jnp
from jax import lax

W = 512
P_SIZE = 4
NRHS = 32
BR = 128
OFF_DEV = 1536
SLOT = 128
K = 2048
RD = 256
OFF = 12288
OFFB = 96
FRONTS = 4
ROWG = 8


def draw_diag_inverse(key, part):
    first_key, second_key = jax.random.split(key)
    shape = (FRONTS, P_SIZE, W, W)
    row_index = lax.broadcasted_iota(jnp.int32, shape, 2)
    col_index = lax.broadcasted_iota(jnp.int32, shape, 3)
    below = jax.random.normal(first_key, shape, jnp.float32)
    diagonal_vals = jax.random.uniform(second_key, shape, jnp.float32, 1.0, 2.0)
    scaled = below * (1.0 / W ** 0.5)
    return jnp.where(row_index > col_index, scaled, jnp.where(row_index == col_index, diagonal_vals, 0.0))


def touch_ends(values, stream_key, least, high):
    shape = values.shape
    place = [jax.random.randint(jax.random.fold_in(stream_key, axis), (), 0, shape[axis]) for axis in range(len(shape))]
    values = values.at[tuple(place)].set(least)
    longest = shape.index(max(shape))
    place[longest] = (place[longest] + 1) % shape[longest]
    return values.at[tuple(place)].set(high)


def levels(key, dims, cuts, low, top_value):
    factor_of = 1.0
    for dim, shards_of in cuts:
        heights = jax.random.uniform(jax.random.fold_in(jax.random.fold_in(key, 6), dim), (shards_of,), jnp.float32, low / len(cuts), top_value / len(cuts))
        factor_of = factor_of * jnp.repeat(jnp.exp(heights), dims[dim] // shards_of).reshape((-1,) + (1,) * (len(dims) - 1 - dim))
    return factor_of


def normal_values(rng, extent, width, limit, cuts=(), kind=jnp.bfloat16):
    level = levels(rng, extent, cuts, -0.22, 0.18) if cuts else 1.0
    drawn = jax.random.normal(rng, extent, jnp.float32) * width * level
    return jnp.minimum(jnp.maximum(drawn, -limit), limit).astype(kind)


def setup_inputs(seed: int = 0) -> dict:
    arg_keys = jax.random.split(jax.random.key(seed), 9)
    return {
        "rhs_diag": normal_values(arg_keys[0], (FRONTS, NRHS, K), 1.0, 6.0, ((0, 4), (2, 8)), jnp.float32),
        "rhs_off": normal_values(arg_keys[1], (FRONTS, NRHS, OFF), 1.0, 6.0, ((0, 4), (2, 8)), jnp.float32),
        "diag_factor": normal_values(arg_keys[2], (FRONTS, K, K), K ** -0.5, 0.125, ((0, 4), (1, 8)), jnp.float32),
        "off_factor": normal_values(arg_keys[3], (FRONTS, OFF, K), K ** -0.5, 0.125, ((0, 4), (1, 8)), jnp.float32),
        "diag_inverse": draw_diag_inverse(jax.random.fold_in(arg_keys[8], 71), 0),
        "pattern": touch_ends((jax.random.randint(arg_keys[5], (FRONTS, P_SIZE, OFFB), 0, 4) < 3).astype(jnp.int32), jax.random.fold_in(arg_keys[5], 1), 0, 1),
        "upd_vals": normal_values(arg_keys[6], (NRHS, FRONTS, ROWG, FRONTS, ROWG, SLOT), 0.3, 4.0, ((1, 4), (2, 8)), jnp.float32),
        "upd_rows": touch_ends(jax.random.randint(arg_keys[7], (FRONTS, ROWG, FRONTS, ROWG, SLOT), 0, RD + OFF_DEV), jax.random.fold_in(arg_keys[7], 1), 0, (RD + OFF_DEV) - 1).astype(jnp.int32),
    }


def reference(rhs_diag, rhs_off, diag_factor, off_factor, diag_inverse, pattern, upd_vals, upd_rows):
    rows_all = K + OFF
    dst_front = lax.broadcasted_iota(jnp.int32, upd_rows.shape, 0)
    dst_group = lax.broadcasted_iota(jnp.int32, upd_rows.shape, 1)
    global_row = jnp.where(upd_rows < RD, dst_group * RD + upd_rows, K + dst_group * OFF_DEV + upd_rows - RD)
    flat_target = (dst_front * rows_all + global_row).reshape(-1).astype(jnp.int32)
    values = jnp.transpose(upd_vals, (0, 3, 4, 1, 2, 5)).reshape(NRHS, -1)
    whole = jnp.concatenate([rhs_diag, rhs_off], axis=2)
    flat_rhs = jnp.transpose(whole, (1, 0, 2)).reshape(NRHS, -1)
    flat_rhs = flat_rhs.at[:, flat_target].add(values)
    whole = jnp.transpose(flat_rhs.reshape(NRHS, FRONTS, rows_all), (1, 0, 2))
    upper = whole[:, :, :K]
    lower = whole[:, :, K:]
    highest = lax.Precision.HIGHEST
    pieces = []
    for panel in range(P_SIZE):
        panel_rhs = upper[:, :, panel * W:(panel + 1) * W]
        piece = jnp.einsum("fnb,fab->fna", panel_rhs, diag_inverse[:, panel], precision=highest)
        pieces.append(piece)
        upper = upper - jnp.einsum("fna,fca->fnc", piece, diag_factor[:, :, panel * W:(panel + 1) * W], precision=highest)
        mask_rows = jnp.repeat(pattern[:, panel, :].astype(jnp.float32), BR, axis=1)
        term = jnp.einsum("fna,fca->fnc", piece, off_factor[:, :, panel * W:(panel + 1) * W], precision=highest)
        lower = lower - term * mask_rows[:, None, :]
    return jnp.concatenate(pieces, axis=2), lower
```

```python
import functools

import jax
import jax.numpy as jnp
from jax import lax
from jax.experimental import pallas as pl
from jax.experimental.pallas import tpu as pltpu
from jax.sharding import PartitionSpec as P

W = 512
BR = 128
MESH = pl.DeviceIdType.MESH
NT = (((1,), (1,)), ((), ()))


def split(x):
    hi = x.astype(jnp.bfloat16)
    lo = (x - hi.astype(jnp.float32)).astype(jnp.bfloat16)
    return hi, lo


def dot_nt(a, b):
    return lax.dot_general(a, b, NT, preferred_element_type=jnp.float32)


def dot3(a2, b_hi, b_lo):
    n = a2.shape[0] // 2
    top = dot_nt(a2, b_hi)
    return top[:n] + top[n:] + dot_nt(a2[:n], b_lo)


def kernel(nf, nr, rd_ref, ro_ref, diag_hbm, off_hbm, inv_hbm, pat_ref, vals_hbm, rows_ref,
           solved_ref, rem_ref,
           diag_f, off_f, inv_f, diag_h, diag_l, off_h, off_l, inv_h, inv_l,
           recv, vs, upper, rhsbuf, load_sem, own_sem, a2a_send, a2a_recv, pan_send, pan_recv):
    f = lax.axis_index("front")
    r = lax.axis_index("row")
    devices = nf * nr
    nrhs, rd = upper.shape
    od = off_f.shape[0]
    panels = inv_f.shape[0]
    per = W // rd
    slot = recv.shape[3]

    load_inv = pltpu.make_async_copy(inv_hbm.at[0], inv_f, load_sem.at[0])
    load_diag = pltpu.make_async_copy(diag_hbm.at[0], diag_f, load_sem.at[1])
    load_off = pltpu.make_async_copy(off_hbm.at[0], off_f, load_sem.at[2])

    def peer(d):
        return lax.rem(f + d // nr, nf), lax.rem(r + lax.rem(d, nr), nr)

    barrier = pltpu.get_barrier_semaphore()

    def greet(d, c):
        pf, pr = peer(d)
        pl.semaphore_signal(barrier, inc=1, device_id=(pf, pr), device_id_type=MESH)
        return c

    lax.fori_loop(1, devices, greet, 0)
    load_inv.start()
    load_diag.start()
    load_off.start()
    own = pltpu.make_async_copy(vals_hbm.at[f, r], recv.at[f, r], own_sem)
    own.start()
    pl.semaphore_wait(barrier, devices - 1)

    def exchange(d):
        pf, pr = peer(d)
        return pltpu.make_async_remote_copy(
            src_ref=vals_hbm.at[pf, pr],
            dst_ref=recv.at[f, r],
            send_sem=a2a_send.at[d],
            recv_sem=a2a_recv.at[d],
            device_id=(pf, pr),
            device_id_type=MESH,
        )

    def send(d, c):
        exchange(d).start()
        return c

    lax.fori_loop(1, devices, send, 0)

    load_inv.wait()
    for p in range(panels):
        def split_inv(i, c, p=p):
            at = pl.ds(pl.multiple_of(i * 64, 64), 64)
            hi, lo = split(inv_f[p, at, :])
            inv_h[p, at, :] = hi
            inv_l[p, at, :] = lo
            return c

        lax.fori_loop(0, W // 64, split_inv, 0)
    load_diag.wait()

    def split_diag(i, c):
        at = pl.ds(pl.multiple_of(i * 16, 16), 16)
        hi, lo = split(diag_f[at, :])
        diag_h[at, :] = hi
        diag_l[at, :] = lo
        return c

    lax.fori_loop(0, rd // 16, split_diag, 0)
    load_off.wait()

    def split_off(i, c):
        at = pl.ds(pl.multiple_of(i * 16, 16), 16)
        hi, lo = split(off_f[at, :])
        off_h[at, :] = hi
        off_l[at, :] = lo
        return c

    lax.fori_loop(0, od // 16, split_off, 0)

    own.wait()

    def arrive(d, c):
        exchange(d).wait_recv()
        return c

    lax.fori_loop(1, devices, arrive, 0)

    for sf in range(nf):
        def split_vals(sr, c, sf=sf):
            hi, lo = split(recv[sf, sr])
            at = pl.ds(pl.multiple_of((sf * nr + sr) * slot, slot), slot)
            vs[pl.ds(0, nrhs), at] = hi
            vs[pl.ds(nrhs, nrhs), at] = lo
            return c

        lax.fori_loop(0, nr, split_vals, 0)

    group = 4

    def scatter(first, count):
        ids = first + lax.broadcasted_iota(jnp.int32, (count, slot), 0)

        def step(k, acc):
            rows = rows_ref[pl.ds(k * group, group), :]
            hot = jnp.concatenate(
                [jnp.where(rows[g:g + 1, :] == ids, 1.0, 0.0).astype(jnp.bfloat16) for g in range(group)], axis=1)
            at = pl.ds(pl.multiple_of(k * group * slot, group * slot), group * slot)
            return acc + dot_nt(vs[:, at], hot)

        acc = lax.fori_loop(0, devices // group, step, jnp.zeros((2 * nrhs, count), jnp.float32))
        return acc[:nrhs] + acc[nrhs:]

    upper[...] = rd_ref[0] + scatter(0, rd)

    chunk = 2 * BR
    chunks = od // chunk

    def scatter_lower(i, c):
        base = pl.multiple_of(i * chunk, chunk)
        at = pl.ds(base, chunk)
        rem_ref[0, :, at] = ro_ref[0, :, at] + scatter(rd + base, chunk)
        return c

    def off_update(p, piece2):
        def step(i, c):
            at = pl.ds(pl.multiple_of(i * chunk, chunk), chunk)
            columns = pl.ds(p * W, W)
            term = dot3(piece2, off_h[at, columns], off_l[at, columns])
            scaled = jnp.concatenate(
                [term[:, b * BR:(b + 1) * BR] * pat_ref[0, p, 2 * i + b].astype(jnp.float32) for b in range(2)], axis=1)
            rem_ref[0, :, at] -= scaled
            return c

        lax.fori_loop(0, chunks, step, 0)

    def share(d):
        return pltpu.make_async_remote_copy(
            src_ref=rhsbuf.at[r],
            dst_ref=rhsbuf.at[r],
            send_sem=pan_send.at[d],
            recv_sem=pan_recv.at[r],
            device_id=(f, lax.rem(r + d, nr)),
            device_id_type=MESH,
        )

    piece2 = None
    for p in range(panels):
        @pl.when(r // per == p)
        def _():
            rhsbuf[r] = upper[...]

            def start(d, c):
                share(d).start()
                return c

            lax.fori_loop(1, nr, start, 0)

        if p == 0:
            lax.fori_loop(0, chunks, scatter_lower, 0)
        else:
            off_update(p - 1, piece2)

        for j in range(p * per, (p + 1) * per):
            @pl.when(r != j)
            def _(j=j):
                pltpu.make_async_remote_copy(
                    src_ref=rhsbuf.at[j],
                    dst_ref=rhsbuf.at[j],
                    send_sem=pan_send.at[0],
                    recv_sem=pan_recv.at[j],
                    device_id=(f, j),
                    device_id_type=MESH,
                ).wait_recv()

        panel_rhs = jnp.concatenate([rhsbuf[j] for j in range(p * per, (p + 1) * per)], axis=1)
        piece = dot3(jnp.concatenate(split(panel_rhs), axis=0), inv_h[p], inv_l[p])
        piece2 = jnp.concatenate(split(piece), axis=0)
        if p < panels - 1:
            @pl.when(r // per > p)
            def _(piece2=piece2, p=p):
                columns = pl.ds(p * W, W)
                upper[...] -= dot3(piece2, diag_h[:, columns], diag_l[:, columns])

        for i in range(per):
            @pl.when(r == p * per + i)
            def _(i=i, piece=piece):
                solved_ref[0] = piece[:, i * rd:(i + 1) * rd]

    off_update(panels - 1, piece2)

    def sent(d, c):
        exchange(d).wait_send()
        return c

    lax.fori_loop(1, devices, sent, 0)

    def shared(d, c):
        share(d).wait_send()
        return c

    lax.fori_loop(1, nr, shared, 0)


def local(nf, nr, rhs_diag, rhs_off, diag_factor, off_factor, diag_inverse, pattern, upd_vals, upd_rows):
    nrhs = upd_vals.shape[0]
    slot = upd_vals.shape[5]
    rd = diag_factor.shape[1]
    od = off_factor.shape[1]
    k = diag_factor.shape[2]
    panels = diag_inverse.shape[1]
    devices = nf * nr
    vals = jnp.transpose(upd_vals[:, 0, 0], (1, 2, 0, 3))
    rows = upd_rows.reshape(devices, slot)
    vmem = pl.BlockSpec(memory_space=pltpu.VMEM)
    anywhere = pl.BlockSpec(memory_space=pl.ANY)
    f32, bf16 = jnp.float32, jnp.bfloat16
    return pl.pallas_call(
        functools.partial(kernel, nf, nr),
        out_shape=(
            jax.ShapeDtypeStruct((1, nrhs, rd), f32),
            jax.ShapeDtypeStruct((1, nrhs, od), f32),
        ),
        in_specs=[vmem, vmem, anywhere, anywhere, anywhere,
                  pl.BlockSpec(memory_space=pltpu.SMEM), anywhere, vmem],
        out_specs=(vmem, vmem),
        scratch_shapes=[
            pltpu.VMEM((rd, k), f32),
            pltpu.VMEM((od, k), f32),
            pltpu.VMEM((panels, W, W), f32),
            pltpu.VMEM((rd, k), bf16),
            pltpu.VMEM((rd, k), bf16),
            pltpu.VMEM((od, k), bf16),
            pltpu.VMEM((od, k), bf16),
            pltpu.VMEM((panels, W, W), bf16),
            pltpu.VMEM((panels, W, W), bf16),
            pltpu.VMEM((nf, nr, nrhs, slot), f32),
            pltpu.VMEM((2 * nrhs, devices * slot), bf16),
            pltpu.VMEM((nrhs, rd), f32),
            pltpu.VMEM((nr, nrhs, rd), f32),
            pltpu.SemaphoreType.DMA((3,)),
            pltpu.SemaphoreType.DMA,
            pltpu.SemaphoreType.DMA((devices,)),
            pltpu.SemaphoreType.DMA((devices,)),
            pltpu.SemaphoreType.DMA((nr,)),
            pltpu.SemaphoreType.DMA((nr,)),
        ],
        compiler_params=pltpu.CompilerParams(
            collective_id=0, has_side_effects=True, vmem_limit_bytes=58 * 1024 * 1024),
    )(rhs_diag, rhs_off, diag_factor, off_factor, diag_inverse, pattern, vals, rows)


def solution(mesh):
    in_specs = (
        P("front", None, "row"),
        P("front", None, "row"),
        P("front", "row", None),
        P("front", "row", None),
        P("front", None, None, None),
        P("front", None, "row"),
        P(None, "front", "row", None, None, None),
        P("front", "row", None, None, None),
    )
    out_specs = (P("front", None, "row"), P("front", None, "row"))
    body = functools.partial(local, mesh.shape["front"], mesh.shape["row"])
    return jax.shard_map(body, mesh=mesh, in_specs=in_specs, out_specs=out_specs, check_vma=False)
```

```python
import functools

import jax
import jax.numpy as jnp
from jax import lax
from jax.experimental import pallas as pl
from jax.experimental.pallas import tpu as pltpu
from jax.sharding import PartitionSpec as P

W = 512
BR = 128
MESH = pl.DeviceIdType.MESH
PART = 256
NT = (((1,), (1,)), ((), ()))


def split(x):
    hi = x.astype(jnp.bfloat16)
    lo = (x - hi.astype(jnp.float32)).astype(jnp.bfloat16)
    return hi, lo


def dot_nt(a, b):
    return lax.dot_general(a, b, NT, preferred_element_type=jnp.float32)


def dot3(a2, b_hi, b_lo):
    n = a2.shape[0] // 2
    top = dot_nt(a2, b_hi)
    return top[:n] + top[n:] + dot_nt(a2[:n], b_lo)


def kernel(nf, nr, rd_ref, ro_ref, diag_hbm, off_hbm, inv_hbm, pat_ref, vals_hbm, rows_ref,
           solved_ref, rem_ref,
           diag_f, off_f, inv_f, diag_h, diag_l, off_h, off_l, inv_h, inv_l,
           recv, vs, hot, code_ref, low_acc, upper, rhsbuf, load_sem, own_sem, a2a_send, a2a_recv, pan_send, pan_recv):
    f = lax.axis_index("front")
    r = lax.axis_index("row")
    devices = nf * nr
    nrhs, rd = upper.shape
    od = off_f.shape[0]
    panels = inv_f.shape[0]
    per = W // rd
    slot = recv.shape[3]

    load_inv = pltpu.make_async_copy(inv_hbm.at[0], inv_f, load_sem.at[0])
    load_diag = pltpu.make_async_copy(diag_hbm.at[0], diag_f, load_sem.at[1])
    load_off = pltpu.make_async_copy(off_hbm.at[0], off_f, load_sem.at[2])

    def peer(d):
        return lax.rem(f + d // nr, nf), lax.rem(r + lax.rem(d, nr), nr)

    barrier = pltpu.get_barrier_semaphore()

    def greet(d, c):
        pf, pr = peer(d)
        pl.semaphore_signal(barrier, inc=1, device_id=(pf, pr), device_id_type=MESH)
        return c

    lax.fori_loop(1, devices, greet, 0)
    load_inv.start()
    load_diag.start()
    load_off.start()
    own = pltpu.make_async_copy(vals_hbm.at[:, f, r, :], recv.at[f, r], own_sem)
    own.start()
    pl.semaphore_wait(barrier, devices - 1)

    def exchange(d):
        pf, pr = peer(d)
        return pltpu.make_async_remote_copy(
            src_ref=vals_hbm.at[:, pf, pr, :],
            dst_ref=recv.at[f, r],
            send_sem=a2a_send.at[d],
            recv_sem=a2a_recv.at[d],
            device_id=(pf, pr),
            device_id_type=MESH,
        )

    def send(d, c):
        exchange(d).start()
        return c

    lax.fori_loop(1, devices, send, 0)

    code_ref[...] = rows_ref[...] + (PART - rd)

    def mark(s, c):
        low = code_ref[pl.ds(s, 1), :] & (PART - 1)
        ids = lax.broadcasted_iota(jnp.int32, (PART, slot), 0)
        at = pl.ds(pl.multiple_of(s * slot, slot), slot)
        hot[:, at] = jnp.where(low == ids, 1.0, 0.0).astype(jnp.bfloat16)
        return c

    lax.fori_loop(0, devices, mark, 0)

    load_inv.wait()
    for p in range(panels):
        def split_inv(i, c, p=p):
            at = pl.ds(pl.multiple_of(i * 64, 64), 64)
            hi, lo = split(inv_f[p, at, :])
            inv_h[p, at, :] = hi
            inv_l[p, at, :] = lo
            return c

        lax.fori_loop(0, W // 64, split_inv, 0)
    load_diag.wait()

    def split_diag(i, c):
        at = pl.ds(pl.multiple_of(i * 16, 16), 16)
        hi, lo = split(diag_f[at, :])
        diag_h[at, :] = hi
        diag_l[at, :] = lo
        return c

    lax.fori_loop(0, rd // 16, split_diag, 0)
    load_off.wait()

    def split_off(i, c):
        at = pl.ds(pl.multiple_of(i * 16, 16), 16)
        hi, lo = split(off_f[at, :])
        off_h[at, :] = hi
        off_l[at, :] = lo
        return c

    lax.fori_loop(0, od // 16, split_off, 0)

    own.wait()

    def arrive(d, c):
        exchange(d).wait_recv()
        return c

    lax.fori_loop(1, devices, arrive, 0)

    for sf in range(nf):
        def split_vals(sr, c, sf=sf):
            hi, lo = split(recv[sf, sr])
            at = pl.ds(pl.multiple_of((sf * nr + sr) * slot, slot), slot)
            vs[pl.ds(0, nrhs), at] = hi
            vs[pl.ds(nrhs, nrhs), at] = lo
            return c

        lax.fori_loop(0, nr, split_vals, 0)

    group = 4
    span = group * slot

    def picked(k, parts):
        block = code_ref[pl.ds(k * group, group), :]
        part = jnp.concatenate([block[g:g + 1, :] for g in range(group)], axis=1) >> 8
        values = vs[:, pl.ds(pl.multiple_of(k * span, span), span)]
        rows = []
        for h in parts:
            mask = jnp.where(jnp.broadcast_to(part, (16, span)) == h, 1.0, 0.0).astype(jnp.bfloat16)
            rows.append(values * jnp.concatenate([mask] * (2 * nrhs // 16), axis=0))
        return jnp.concatenate(rows, axis=0)

    def reduced(acc, h):
        return acc[2 * h * nrhs:(2 * h + 1) * nrhs] + acc[(2 * h + 1) * nrhs:(2 * h + 2) * nrhs]

    steps = devices // group
    unroll = 8

    def upper_step(i, acc):
        for u in range(unroll):
            k = i * unroll + u
            acc = acc + dot_nt(picked(k, [0]), hot[:, pl.ds(pl.multiple_of(k * span, span), span)])
        return acc

    acc = lax.fori_loop(0, steps // unroll, upper_step, jnp.zeros((2 * nrhs, PART), jnp.float32))
    upper[...] = rd_ref[0] + reduced(acc, 0)[:, PART - rd:]

    chunk = 2 * BR
    chunks = od // chunk
    parts = list(range(1, chunks + 1))

    def scatter_lower():
        low_acc[...] = jnp.zeros_like(low_acc)

        def step(k, c):
            low_acc[...] += dot_nt(picked(k, parts), hot[:, pl.ds(pl.multiple_of(k * span, span), span)])
            return c

        lax.fori_loop(0, steps, step, 0)
        for h in range(chunks):
            at = pl.ds(h * chunk, chunk)
            rem_ref[0, :, at] = ro_ref[0, :, at] + reduced(low_acc, h)

    def off_update(p, piece2):
        def step(i, c):
            at = pl.ds(pl.multiple_of(i * chunk, chunk), chunk)
            columns = pl.ds(p * W, W)
            term = dot3(piece2, off_h[at, columns], off_l[at, columns])
            scaled = jnp.concatenate(
                [term[:, b * BR:(b + 1) * BR] * pat_ref[0, p, 2 * i + b].astype(jnp.float32) for b in range(2)], axis=1)
            rem_ref[0, :, at] -= scaled
            return c

        lax.fori_loop(0, chunks, step, 0)

    def share(d):
        return pltpu.make_async_remote_copy(
            src_ref=rhsbuf.at[r],
            dst_ref=rhsbuf.at[r],
            send_sem=pan_send.at[d],
            recv_sem=pan_recv.at[r],
            device_id=(f, lax.rem(r + d, nr)),
            device_id_type=MESH,
        )

    piece2 = None
    for p in range(panels):
        @pl.when(r // per == p)
        def _():
            rhsbuf[r] = upper[...]

            def start(d, c):
                share(d).start()
                return c

            lax.fori_loop(1, nr, start, 0)

        if p == 0:
            scatter_lower()
        else:
            off_update(p - 1, piece2)

        for j in range(p * per, (p + 1) * per):
            @pl.when(r != j)
            def _(j=j):
                pltpu.make_async_remote_copy(
                    src_ref=rhsbuf.at[j],
                    dst_ref=rhsbuf.at[j],
                    send_sem=pan_send.at[0],
                    recv_sem=pan_recv.at[j],
                    device_id=(f, j),
                    device_id_type=MESH,
                ).wait_recv()

        panel_rhs = jnp.concatenate([rhsbuf[j] for j in range(p * per, (p + 1) * per)], axis=1)
        piece = dot3(jnp.concatenate(split(panel_rhs), axis=0), inv_h[p], inv_l[p])
        piece2 = jnp.concatenate(split(piece), axis=0)
        if p < panels - 1:
            @pl.when(r // per > p)
            def _(piece2=piece2, p=p):
                columns = pl.ds(p * W, W)
                upper[...] -= dot3(piece2, diag_h[:, columns], diag_l[:, columns])

        for i in range(per):
            @pl.when(r == p * per + i)
            def _(i=i, piece=piece):
                solved_ref[0] = piece[:, i * rd:(i + 1) * rd]

    off_update(panels - 1, piece2)

    def sent(d, c):
        exchange(d).wait_send()
        return c

    lax.fori_loop(1, devices, sent, 0)

    def shared(d, c):
        share(d).wait_send()
        return c

    lax.fori_loop(1, nr, shared, 0)


def local(nf, nr, rhs_diag, rhs_off, diag_factor, off_factor, diag_inverse, pattern, upd_vals, upd_rows):
    nrhs = upd_vals.shape[0]
    slot = upd_vals.shape[5]
    rd = diag_factor.shape[1]
    od = off_factor.shape[1]
    k = diag_factor.shape[2]
    panels = diag_inverse.shape[1]
    devices = nf * nr
    vals = upd_vals.reshape(upd_vals.shape[0], nf, nr, slot)
    rows = upd_rows.reshape(devices, slot)
    vmem = pl.BlockSpec(memory_space=pltpu.VMEM)
    anywhere = pl.BlockSpec(memory_space=pl.ANY)
    f32, bf16 = jnp.float32, jnp.bfloat16
    return pl.pallas_call(
        functools.partial(kernel, nf, nr),
        out_shape=(
            jax.ShapeDtypeStruct((1, nrhs, rd), f32),
            jax.ShapeDtypeStruct((1, nrhs, od), f32),
        ),
        in_specs=[vmem, vmem, anywhere, anywhere, anywhere,
                  pl.BlockSpec(memory_space=pltpu.SMEM), anywhere, vmem],
        out_specs=(vmem, vmem),
        scratch_shapes=[
            pltpu.VMEM((rd, k), f32),
            pltpu.VMEM((od, k), f32),
            pltpu.VMEM((panels, W, W), f32),
            pltpu.VMEM((rd, k), bf16),
            pltpu.VMEM((rd, k), bf16),
            pltpu.VMEM((od, k), bf16),
            pltpu.VMEM((od, k), bf16),
            pltpu.VMEM((panels, W, W), bf16),
            pltpu.VMEM((panels, W, W), bf16),
            pltpu.VMEM((nf, nr, nrhs, slot), f32),
            pltpu.VMEM((2 * nrhs, devices * slot), bf16),
            pltpu.VMEM((PART, devices * slot), bf16),
            pltpu.VMEM((devices, slot), jnp.int32),
            pltpu.VMEM((2 * nrhs * od // PART, PART), f32),
            pltpu.VMEM((nrhs, rd), f32),
            pltpu.VMEM((nr, nrhs, rd), f32),
            pltpu.SemaphoreType.DMA((3,)),
            pltpu.SemaphoreType.DMA,
            pltpu.SemaphoreType.DMA((devices,)),
            pltpu.SemaphoreType.DMA((devices,)),
            pltpu.SemaphoreType.DMA((nr,)),
            pltpu.SemaphoreType.DMA((nr,)),
        ],
        compiler_params=pltpu.CompilerParams(
            collective_id=0, has_side_effects=True, vmem_limit_bytes=58 * 1024 * 1024),
    )(rhs_diag, rhs_off, diag_factor, off_factor, diag_inverse, pattern, vals, rows)


def solution(mesh):
    in_specs = (
        P("front", None, "row"),
        P("front", None, "row"),
        P("front", "row", None),
        P("front", "row", None),
        P("front", None, None, None),
        P("front", None, "row"),
        P(None, "front", "row", None, None, None),
        P("front", "row", None, None, None),
    )
    out_specs = (P("front", None, "row"), P("front", None, "row"))
    body = functools.partial(local, mesh.shape["front"], mesh.shape["row"])
    return jax.shard_map(body, mesh=mesh, in_specs=in_specs, out_specs=out_specs, check_vma=False)
```
